32 devices in a mesh: member: 2 (over y), polar: 4 (over z), azimuth: 4 (over x, core).
Axes of the slice: x: 2, y: 2, z: 4, core: 2. Of those that a mesh axis runs over, the one named last changes fastest.
Arguments:
- conv_out: bfloat16 [32, 720, 640], P(('member', 'polar'), 'azimuth'), parts along dimension 0, may hold values from -6 to 6
- grad_out: bfloat16 [32, 720, 640], P(('member', 'polar'), 'azimuth'), parts along dimension 0, may hold values from -6 to 6
- w_in: bfloat16 [640, 1280], replicated, may hold values from -0.25 to 0.25
- b_in: float32 [1280], replicated, may hold values from -4 to 4
- w_out: bfloat16 [1280, 640], replicated, may hold values from -0.15625 to 0.15625
- basis_weight: float32 [9, 640], replicated, may hold values from -1 to 1
- filt: bfloat16 [9, 16, 640], replicated, may hold values from -2 to 2
- offsets: int32 [16, 9], replicated, may hold values from 0 to 15, as said below
Outputs:
- grad_in: bfloat16 [32, 720, 640], P(('member', 'polar'), 'azimuth'), parts along dimension 0
The draws below stay inside these ranges and needn't reach their ends.
There are 2 independent parts, one for each index of `member`. The reference program is written for one: setup_inputs(seed, part) draws one part's arguments, and reference() takes and returns one part's arrays. A program takes and returns all parts, laid end to end along the dimension named above; an argument that names none is the same for every part. Nothing has to cross between parts.
Inputs may be any that keep to these rules, and one draw needn't show every extreme that they name: offsets[i, k] lies within 3 rows of i; column 0 is i, column 1 is min(i + 3, 15), column 2 is max(i - 3, 0).
All inputs are finite; a program needn't handle non-finite values.
Results may differ from the reference program's by a relative error of at most 0.006.
Values may be sent and summed in bfloat16 or wider, within the bound.
A program may use at most 64 MiB of HBM per device.

```python
import math
import jax
import jax.numpy as jnp
from jax import lax

CHANNELS = 640
HIDDEN_SIZE = 1280
NLON = 720
MODES = 320
BASES = 9
REACH = 3
NLAT = 16


def draw_offsets(key, part):
    rows = jnp.arange(NLAT, dtype=jnp.int32)[:, None]
    column = jnp.arange(BASES, dtype=jnp.int32)[None, :]
    drawn = jax.random.randint(jax.random.fold_in(key, 17), (NLAT, BASES), -REACH, REACH + 1, dtype=jnp.int32)
    shift_rows = jnp.where(column == 0, 0, jnp.where(column == 1, REACH, jnp.where(column == 2, -REACH, drawn)))
    return jnp.clip(rows + shift_rows, 0, NLAT - 1).astype(jnp.int32)


def shard_levels(stream_key, shape, shards, low, largest):
    gain = 1.0
    for axis_at, blocks in shards:
        draws = jax.random.uniform(jax.random.fold_in(jax.random.fold_in(stream_key, 6), axis_at), (blocks,), jnp.float32, low / len(shards), largest / len(shards))
        gain = gain * jnp.repeat(jnp.exp(draws), shape[axis_at] // blocks).reshape((-1,) + (1,) * (len(shape) - 1 - axis_at))
    return gain


def normal_values(key, dims, scale, limit, pieces=(), held_as=jnp.bfloat16):
    values = scale * jax.random.normal(key, dims, jnp.float32)
    if pieces:
        values = values * shard_levels(key, dims, pieces, -0.22, 0.18)
    return jnp.clip(values, -limit, limit).astype(held_as)


def setup_inputs(seed: int = 0, part: int = 0) -> dict:
    key_list = jax.random.split(jax.random.key(seed), 9)
    part_keys = jax.random.split(jax.random.fold_in(key_list[8], part), 9)
    conv_out = normal_values(part_keys[0], (NLAT, NLON, CHANNELS), 1.0, 6.0, ((0, 4), (1, 4)))
    grad_out = normal_values(part_keys[1], (NLAT, NLON, CHANNELS), 1.0, 6.0, ((0, 4), (1, 4)))
    w_in = normal_values(key_list[2], (CHANNELS, HIDDEN_SIZE), CHANNELS ** -0.5, 0.25)
    b_in = normal_values(key_list[3], (HIDDEN_SIZE,), 1.0, 4.0, (), jnp.float32)
    w_out = normal_values(key_list[4], (HIDDEN_SIZE, CHANNELS), HIDDEN_SIZE ** -0.5, 0.15625)
    basis_weight = jnp.clip(jax.random.uniform(key_list[5], (BASES, CHANNELS), jnp.float32, -1.0, 1.0), -1.0, 1.0)
    filt = normal_values(key_list[6], (BASES, NLAT, 2 * MODES), 0.33, 2.0)
    offsets = draw_offsets(jax.random.fold_in(key_list[8], 71), part)
    return {"conv_out": conv_out, "grad_out": grad_out, "w_in": w_in, "b_in": b_in, "w_out": w_out, "basis_weight": basis_weight, "filt": filt, "offsets": offsets}


def gelu_slope(values):
    normal_cdf = 0.5 * (1.0 + jax.scipy.special.erf(values / math.sqrt(2.0)))
    density = jnp.exp(-0.5 * values * values) / math.sqrt(2.0 * math.pi)
    return normal_cdf + values * density

def fourier_tables(length, modes):
    positions = jnp.arange(length, dtype=jnp.int32)
    waves = jnp.arange(modes, dtype=jnp.int32)
    phase = positions[:, None] * waves[None, :] % length
    angle = 2.0 * math.pi / length * phase.astype(jnp.float32)
    scale = 1.0 / math.sqrt(length)
    factor = jnp.where(waves == 0, 1.0, 2.0).astype(jnp.float32)
    analysis = (jnp.concatenate([jnp.cos(angle), -jnp.sin(angle)], axis=1) * scale).astype(jnp.bfloat16)
    synth = jnp.concatenate([jnp.cos(angle) * factor[None, :], -jnp.sin(angle) * factor[None, :]], axis=1) * scale
    return (analysis, jnp.transpose(synth).astype(jnp.bfloat16))

def spectral_term(spectrum, psi, weight):
    half = psi.shape[-1] // 2
    psi_full = psi.astype(jnp.float32)
    psi_real = psi_full[:, None, :half]
    psi_imag = psi_full[:, None, half:]
    spec_real = spectrum[:, :, :half]
    spec_imag = spectrum[:, :, half:]
    real_part = psi_real * spec_real + psi_imag * spec_imag
    imag_part = psi_real * spec_imag - psi_imag * spec_real
    return jnp.concatenate([real_part, imag_part], axis=2) * weight[None, :, None]

def reference(conv_out, grad_out, w_in, b_in, w_out, basis_weight, filt, offsets):

    def mlp_row(pair):
        h_row, g_row = pair
        pre = jnp.dot(h_row, w_in, preferred_element_type=jnp.float32) + b_in[None, :]
        back = lax.dot_general(g_row, w_out, (((1,), (1,)), ((), ())), preferred_element_type=jnp.float32)
        slope_grad = (back * gelu_slope(pre)).astype(jnp.bfloat16)
        hidden = lax.dot_general(slope_grad, w_in, (((1,), (1,)), ((), ())), preferred_element_type=jnp.float32)
        return hidden.astype(jnp.bfloat16)
    hidden_grad = lax.map(mlp_row, (conv_out, grad_out))
    hidden_grad = lax.optimization_barrier(hidden_grad)
    analysis, synthesis = fourier_tables(NLON, MODES)
    spectrum = jnp.einsum('inc,nm->icm', hidden_grad.astype(jnp.float32), analysis.astype(jnp.float32), precision=lax.Precision.HIGHEST)
    outspec = jnp.zeros(spectrum.shape, jnp.float32)
    for basis in range(BASES):
        contrib = spectral_term(spectrum, filt[basis], basis_weight[basis])
        outspec = outspec.at[offsets[:, basis]].add(contrib)
    rounded = lax.optimization_barrier(outspec.astype(jnp.bfloat16))
    conv_grad = jnp.einsum('jcm,mn->jnc', rounded.astype(jnp.float32), synthesis.astype(jnp.float32), precision=lax.Precision.HIGHEST).astype(jnp.bfloat16)
    return (grad_out.astype(jnp.float32) + conv_grad.astype(jnp.float32)).astype(jnp.bfloat16)
```

```python
import functools
import math

import jax
import jax.numpy as jnp
import ml_dtypes
import numpy as np
from jax import lax
from jax.experimental import pallas as pl
from jax.experimental.pallas import tpu as pltpu
from jax.sharding import PartitionSpec as P

REACH = 3
LANES = 128
SHIFTS = 2 * REACH + 1
MESH = pl.DeviceIdType.MESH
F32 = jnp.float32
BF16 = jnp.bfloat16


def fourier_tables(length, modes):
    phase = np.arange(length)[:, None] * np.arange(modes)[None, :] % length
    angle = 2.0 * math.pi / length * phase
    scale = 1.0 / math.sqrt(length)
    factor = np.where(np.arange(modes) == 0, 1.0, 2.0)[None, :]
    analysis = np.concatenate([np.cos(angle), -np.sin(angle)], axis=1) * scale
    synth = np.concatenate([np.cos(angle) * factor, -np.sin(angle) * factor], axis=1) * scale
    return analysis, synth


def gelu_slope(values):
    normal_cdf = 0.5 * (1.0 + lax.erf(values * (1.0 / math.sqrt(2.0))))
    density = jnp.exp(-0.5 * values * values) * (1.0 / math.sqrt(2.0 * math.pi))
    return normal_cdf + values * density


def dot(a, b):
    return jnp.dot(a, b, preferred_element_type=F32)


def dot_nt(a, b):
    return lax.dot_general(a, b, (((1,), (1,)), ((), ())), preferred_element_type=F32)


def exchange_groups(blocks):
    count = len(blocks)
    group = LANES // count
    lane_group = lax.broadcasted_iota(jnp.int32, blocks[0].shape, 1) // group
    skewed = [blocks[0]] + [pltpu.roll(blocks[r], r * group, 1) for r in range(1, count)]
    result = []
    for p in range(count):
        value = skewed[0]
        for r in range(1, count):
            value = jnp.where(lane_group == (p + r) % count, skewed[r], value)
        if p > 0:
            value = pltpu.roll(value, LANES - p * group, 1)
        result.append(value)
    return result


def kernel(
    parts, bands, conv_at, grad_at, w_in_at, b_in, w_out_at, weight, filt, offsets, ana_at, syn_at,
    out,
    conv_n, grad_n, conv, grad, w_in, w_out, ana, syn, slope, send, recv, spec, z_out, z_low, z_high, low, high,
    gain, flipped, wlines, outspec, ret_send, ret_recv,
    a_send, a_recv, z_send, z_recv, r_send, r_recv, loads,
):
    lon, rows, channels = conv_n.shape
    hidden = w_in.shape[1]
    tiles = channels // LANES
    group = LANES // rows
    pad = conv.shape[0] // rows
    me = lax.axis_index("azimuth")
    band = lax.axis_index("polar")
    bases, lat, modes2 = filt.shape
    modes = modes2 // 2
    width = rows + 2 * REACH
    rest = modes2 // rows
    body = modes2 - rest
    has_low = band > 0
    has_high = band < bands - 1

    def peer_of(step):
        base = lax.rem(me + 2 * (step // 2), parts)
        return base + 1 - 2 * lax.rem(base, 2) if step % 2 else base

    steps = list(range(parts // 2, parts)) + list(range(1, parts // 2))
    peers = {step: peer_of(step) for step in steps}

    barrier = pltpu.get_barrier_semaphore()
    for step in steps:
        pl.semaphore_signal(barrier, inc=1, device_id={"azimuth": peers[step]}, device_id_type=MESH)

    @pl.when(has_low)
    def _():
        pl.semaphore_signal(barrier, inc=1, device_id={"polar": band - 1}, device_id_type=MESH)

    @pl.when(has_high)
    def _():
        pl.semaphore_signal(barrier, inc=1, device_id={"polar": band + 1}, device_id_type=MESH)

    piece = 2 * LANES
    pairs = [(conv_at, conv_n), (w_in_at.at[:, 0:piece], w_in.at[:, 0:piece]),
             (grad_at, grad_n), (w_out_at.at[0:piece], w_out.at[0:piece])]
    for at in range(piece, hidden, piece):
        pairs.append((w_in_at.at[:, at : at + piece], w_in.at[:, at : at + piece]))
        pairs.append((w_out_at.at[at : at + piece], w_out.at[at : at + piece]))
    pairs += [(ana_at, ana), (syn_at, syn)]
    copies = [pltpu.make_async_copy(src, dst, loads.at[n]) for n, (src, dst) in enumerate(pairs)]
    for copy in copies:
        copy.start()

    @pl.when(jnp.logical_not(has_low))
    def _():
        z_low[...] = jnp.zeros(z_low.shape, BF16)

    @pl.when(jnp.logical_not(has_high))
    def _():
        z_high[...] = jnp.zeros(z_high.shape, BF16)

    def unweave(src, dst):
        turned = jnp.transpose(src[...], (1, 0, 2))
        for row in range(rows):
            dst[row * pad : row * pad + lon, :] = turned[row]
            dst[row * pad + lon : (row + 1) * pad, :] = jnp.zeros((pad - lon, channels), BF16)

    copies[0].wait()
    unweave(conv_n, conv)
    copies[2].wait()
    unweave(grad_n, grad)
    copies[1].wait()
    copies[3].wait()
    for n, at in enumerate(range(0, hidden, piece)):
        if n > 0:
            copies[2 + 2 * n].wait()
            copies[3 + 2 * n].wait()
        pre = dot(conv[...], w_in[:, at : at + piece]) + b_in[at : at + piece][None, :]
        back = dot_nt(grad[...], w_out[at : at + piece, :])
        slope[:, at : at + piece] = (back * gelu_slope(pre)).astype(BF16)

    neighbours = jnp.where(has_low, 1, 0) + jnp.where(has_high, 1, 0)
    pl.semaphore_wait(barrier, parts - 1 + neighbours)

    def a_copy(step, k, src_at, dst_at):
        return pltpu.make_async_remote_copy(
            src_ref=send.at[src_at, k], dst_ref=recv.at[k, dst_at],
            send_sem=a_send.at[step, k], recv_sem=a_recv.at[step, k],
            device_id={"azimuth": peers[step]}, device_id_type=MESH,
        )

    def r_copy(step, k, src_at, dst_at):
        return pltpu.make_async_remote_copy(
            src_ref=ret_send.at[src_at, k], dst_ref=ret_recv.at[k, dst_at],
            send_sem=r_send.at[step, k], recv_sem=r_recv.at[step, k],
            device_id={"azimuth": peers[step]}, device_id_type=MESH,
        )

    def up_copy(k):
        return pltpu.make_async_remote_copy(
            src_ref=z_out.at[0, k], dst_ref=z_low.at[k], send_sem=z_send.at[0, k], recv_sem=z_recv.at[0, k],
            device_id={"polar": band + 1}, device_id_type=MESH,
        )

    def down_copy(k):
        return pltpu.make_async_remote_copy(
            src_ref=z_out.at[1, k], dst_ref=z_high.at[k], send_sem=z_send.at[1, k], recv_sem=z_recv.at[1, k],
            device_id={"polar": band - 1}, device_id_type=MESH,
        )

    for k in range(tiles):
        full = dot_nt(slope[...], w_in[k * LANES : (k + 1) * LANES, :])
        mixed = exchange_groups([full[row * pad : (row + 1) * pad] for row in range(rows)])
        for part in range(parts):
            send[part, k] = mixed[part][:lon].astype(BF16)
        for step in steps:
            a_copy(step, k, peers[step], me).start()
        recv[k, me] = send[me, k]

    half = bases * width
    lines = 2 * half

    def line_parts(lanes):
        line = lax.broadcasted_iota(jnp.int32, (lines, lanes), 0)
        low_bits = line >= half
        line = jnp.where(low_bits, line - half, line)
        basis = line // width
        return low_bits, basis, line - basis * width, lax.broadcasted_iota(jnp.int32, (lines, lanes), 1)

    start_lat = band * rows - REACH
    low_bits, basis, place, lane = line_parts(bases * lat)
    pick = jnp.where(lane == basis * lat + place + start_lat, 1.0, 0.0)
    pick = jnp.where((place + start_lat >= 0) & (place + start_lat < lat), pick, 0.0)
    f_t = dot(pick.astype(BF16), filt[...].reshape(bases * lat, modes2))
    flipped[...] = jnp.transpose(f_t).astype(BF16)
    low_bits, basis, place, lane = line_parts(lat)
    pick = jnp.where(lane == place + start_lat, 1.0, 0.0).astype(BF16)
    rows_of = dot(pick, offsets[...].astype(F32).astype(BF16))
    low_bits, basis, place, lane = line_parts(bases)
    goal = jnp.sum(jnp.where(lane == basis, rows_of, 0.0), axis=1, keepdims=True)
    goal = jnp.broadcast_to(goal.astype(jnp.int32) - band * rows, (lines, LANES))
    mine = []
    for k in range(tiles):
        tile = weight[:, k * LANES : (k + 1) * LANES]
        chosen = jnp.concatenate([tile[:, 0:group]] * rows, axis=1)
        for part in range(1, parts):
            spread = jnp.concatenate([tile[:, part * group : (part + 1) * group]] * rows, axis=1)
            chosen = jnp.where(me == part, spread, chosen)
        mine.append(chosen)
    weights = jnp.concatenate(mine, axis=1)
    top = weights.astype(BF16)
    remainder = (weights - top.astype(F32)).astype(BF16)
    chosen = jnp.where(lane == basis, 1.0, 0.0)
    wlines[...] = dot(jnp.where(low_bits, 0.0, chosen).astype(BF16), top) + dot(
        jnp.where(low_bits, chosen, 0.0).astype(BF16), remainder
    )
    low_bits, basis, source, lane = line_parts(LANES)
    lane_row = lane // group
    aim = jnp.where(goal == lane_row, source - lane_row, SHIFTS)

    def make_gain(k):
        scale = wlines[:, k * LANES : (k + 1) * LANES]
        table = jnp.concatenate(
            [jnp.where(aim == shift, scale, 0.0).astype(BF16) for shift in range(SHIFTS)], axis=1
        )
        made = dot(flipped[...], table)
        for shift in range(SHIFTS):
            gain[k * SHIFTS + shift] = made[:, shift * LANES : (shift + 1) * LANES]

    for k in range(tiles):
        make_gain(k)

    def lane_groups(size):
        return lax.broadcasted_iota(jnp.int32, (size, LANES), 1) // group

    def analyze(k):
        if k == 0:
            copies[-2].wait()
        for step in steps:
            a_copy(step, k, peers[step], peers[step]).wait_recv()
        total = dot(ana[0], recv[k, 0])
        for src in range(1, parts):
            total = total + dot(ana[src], recv[k, src])
        spec[k] = total.astype(BF16)
        main, extra = total[:body], total[body:]
        free = lane_groups(rest)
        for g in range(REACH):
            at = slice(g * rest, (g + 1) * rest)
            moved = pltpu.roll(extra, LANES - (g + 1) * group, 1)
            z_out[0, k, at, :] = jnp.where(free == 0, moved, main[at]).astype(BF16)
        for g in range(REACH):
            at = slice(g * rest, (g + 1) * rest)
            moved = pltpu.roll(extra, (REACH - g) * group, 1)
            z_out[1, k, at, :] = jnp.where(free == REACH, moved, main[at]).astype(BF16)

        @pl.when(has_high)
        def _():
            up_copy(k).start()

        @pl.when(has_low)
        def _():
            down_copy(k).start()

    chunk = 64

    def filter_tile(k):
        if k == 0:
            copies[-1].wait()

        @pl.when(has_low)
        def _():
            up_copy(k).wait_recv()

        @pl.when(has_high)
        def _():
            down_copy(k).wait_recv()

        free = lane_groups(rest)
        low[0:body, :] = z_low[k]
        high[0:body, :] = z_high[k]
        tail_low = jnp.zeros((rest, LANES), F32)
        tail_high = jnp.zeros((rest, LANES), F32)
        for g in range(REACH):
            at = slice(g * rest, (g + 1) * rest)
            moved = pltpu.roll(z_low[k, at, :].astype(F32), (g + 1) * group, 1)
            tail_low = jnp.where(free == g + 1, moved, tail_low)
            moved = pltpu.roll(z_high[k, at, :].astype(F32), LANES - (REACH - g) * group, 1)
            tail_high = jnp.where(free == g, moved, tail_high)
        low[body:, :] = tail_low.astype(BF16)
        high[body:, :] = tail_high.astype(BF16)
        lane = lax.broadcasted_iota(jnp.int32, (chunk, LANES), 1)

        def window(below, own, above, shift):
            turn = (REACH - shift) * group
            if turn == 0:
                return own
            if turn > 0:
                return pltpu.roll(jnp.where(lane < LANES - turn, own, below), turn, 1)
            return pltpu.roll(jnp.where(lane >= -turn, own, above), LANES + turn, 1)

        def one(it, carry):
            re = pl.ds(it * chunk, chunk)
            im = pl.ds(modes + it * chunk, chunk)
            real = jnp.zeros((chunk, LANES), F32)
            imag = jnp.zeros((chunk, LANES), F32)
            around_re = [ref[re, :].astype(F32) for ref in (low, spec.at[k], high)]
            around_im = [ref[im, :].astype(F32) for ref in (low, spec.at[k], high)]
            for shift in range(SHIFTS):
                gr, gi = gain[k * SHIFTS + shift, re, :], gain[k * SHIFTS + shift, im, :]
                sr, si = window(*around_re, shift), window(*around_im, shift)
                real = real + gr * sr + gi * si
                imag = imag + gr * si - gi * sr
            outspec[re, :] = real.astype(BF16)
            outspec[im, :] = imag.astype(BF16)
            return carry

        lax.fori_loop(0, modes // chunk, one, 0)
        values = outspec[...]
        for step in steps:
            ret_send[peers[step], k] = dot(syn[peers[step]], values).astype(BF16)
            r_copy(step, k, peers[step], me).start()
        ret_recv[k, me] = dot(syn[me], values).astype(BF16)

    def finish(k):
        for step in steps:
            r_copy(step, k, peers[step], peers[step]).wait_recv()
        sums = exchange_groups([ret_recv[k, src].astype(F32) for src in range(parts)])
        cols = slice(k * LANES, (k + 1) * LANES)
        done = [
            (sums[row] + grad[row * pad : row * pad + lon, cols].astype(F32)).astype(BF16) for row in range(rows)
        ]
        out[:, :, cols] = jnp.transpose(jnp.stack(done, axis=0), (1, 0, 2))

    order = [("a", 0), ("a", 1), ("a", 2), ("f", 0), ("a", 3), ("f", 1), ("a", 4), ("f", 2), ("f", 3), ("e", 0), ("e", 1), ("f", 4), ("e", 2), ("e", 3), ("e", 4)]
    if tiles != 5:
        order = [(what, k) for what in "afe" for k in range(tiles)]
    for what, k in order:
        {"a": analyze, "f": filter_tile, "e": finish}[what](k)

    for k in range(tiles):
        for step in steps:
            a_copy(step, k, peers[step], me).wait_send()
            r_copy(step, k, peers[step], me).wait_send()

        @pl.when(has_high)
        def _():
            up_copy(k).wait_send()

        @pl.when(has_low)
        def _():
            down_copy(k).wait_send()


def on_device(parts, bands, conv_out, grad_out, w_in, b_in, w_out, basis_weight, filt, offsets):
    rows, lon, channels = conv_out.shape
    hidden = w_in.shape[1]
    assert parts == rows == REACH + 1 and LANES % parts == 0 and channels % LANES == 0
    modes2 = filt.shape[2]
    modes = modes2 // 2
    bases, width = filt.shape[0], rows + 2 * REACH
    assert filt.shape[1] <= 256 and modes2 % (16 * rows) == 0 and hidden % (2 * LANES) == 0
    analysis, synth = fourier_tables(parts * lon, modes)
    ana = np.ascontiguousarray(
        analysis.reshape(parts, lon, modes2).transpose(0, 2, 1)
    ).astype(ml_dtypes.bfloat16)
    syn = synth.reshape(parts, lon, modes2).astype(ml_dtypes.bfloat16)
    tiles = channels // LANES
    pad = -(-lon // 16) * 16
    body = modes2 - modes2 // rows
    vmem = pl.BlockSpec(memory_space=pltpu.VMEM)
    hbm = pl.BlockSpec(memory_space=pltpu.HBM)
    dma = pltpu.SemaphoreType.DMA
    result = pl.pallas_call(
        functools.partial(kernel, parts, bands),
        out_shape=jax.ShapeDtypeStruct((lon, rows, channels), BF16),
        in_specs=[hbm, hbm, hbm, vmem, hbm, vmem, vmem, vmem, hbm, hbm],
        out_specs=vmem,
        scratch_shapes=[
            pltpu.VMEM((lon, rows, channels), BF16),
            pltpu.VMEM((lon, rows, channels), BF16),
            pltpu.VMEM((rows * pad, channels), BF16),
            pltpu.VMEM((rows * pad, channels), BF16),
            pltpu.VMEM(w_in.shape, BF16),
            pltpu.VMEM(w_out.shape, BF16),
            pltpu.VMEM(ana.shape, BF16),
            pltpu.VMEM(syn.shape, BF16),
            pltpu.VMEM((rows * pad, hidden), BF16),
            pltpu.VMEM((parts, tiles, lon, LANES), BF16),
            pltpu.VMEM((tiles, parts, lon, LANES), BF16),
            pltpu.VMEM((tiles, modes2, LANES), BF16),
            pltpu.VMEM((2, tiles, body, LANES), BF16),
            pltpu.VMEM((tiles, body, LANES), BF16),
            pltpu.VMEM((tiles, body, LANES), BF16),
            pltpu.VMEM((modes2, LANES), BF16),
            pltpu.VMEM((modes2, LANES), BF16),
            pltpu.VMEM((tiles * SHIFTS, modes2, LANES), F32),
            pltpu.VMEM((modes2, 2 * bases * width), BF16),
            pltpu.VMEM((2 * bases * width, channels), F32),
            pltpu.VMEM((modes2, LANES), BF16),
            pltpu.VMEM((parts, tiles, lon, LANES), BF16),
            pltpu.VMEM((tiles, parts, lon, LANES), BF16),
            dma((parts, tiles)),
            dma((parts, tiles)),
            dma((2, tiles)),
            dma((2, tiles)),
            dma((parts, tiles)),
            dma((parts, tiles)),
            dma((4 + hidden // LANES,)),
        ],
        compiler_params=pltpu.CompilerParams(
            collective_id=0, has_side_effects=True, vmem_limit_bytes=52 * 1024 * 1024
        ),
    )(jnp.transpose(conv_out, (1, 0, 2)), jnp.transpose(grad_out, (1, 0, 2)), w_in, b_in, w_out, basis_weight, filt, offsets,
      jnp.asarray(ana), jnp.asarray(syn))
    return jnp.transpose(result, (1, 0, 2))


def solution(mesh):
    grid = P(("member", "polar"), "azimuth", None)
    return jax.shard_map(
        functools.partial(on_device, mesh.shape["azimuth"], mesh.shape["polar"]),
        mesh=mesh,
        in_specs=(grid, grid, P(), P(), P(), P(), P(), P()),
        out_specs=grid,
        check_vma=False,
    )
```

```python
import functools
import math

import jax
import jax.numpy as jnp
import ml_dtypes
import numpy as np
from jax import lax
from jax.experimental import pallas as pl
from jax.experimental.pallas import tpu as pltpu
from jax.sharding import PartitionSpec as P

REACH = 3
LANES = 128
SHIFTS = 2 * REACH + 1
MESH = pl.DeviceIdType.MESH
F32 = jnp.float32
BF16 = jnp.bfloat16


def fourier_tables(length, modes):
    phase = np.arange(length)[:, None] * np.arange(modes)[None, :] % length
    angle = 2.0 * math.pi / length * phase
    scale = 1.0 / math.sqrt(length)
    factor = np.where(np.arange(modes) == 0, 1.0, 2.0)[None, :]
    analysis = np.concatenate([np.cos(angle), -np.sin(angle)], axis=1) * scale
    synth = np.concatenate([np.cos(angle) * factor, -np.sin(angle) * factor], axis=1) * scale
    return analysis, synth


def gelu_slope(values):
    normal_cdf = 0.5 * (1.0 + lax.erf(values * (1.0 / math.sqrt(2.0))))
    density = jnp.exp(-0.5 * values * values) * (1.0 / math.sqrt(2.0 * math.pi))
    return normal_cdf + values * density


def dot(a, b):
    return jnp.dot(a, b, preferred_element_type=F32)


def dot_nt(a, b):
    return lax.dot_general(a, b, (((1,), (1,)), ((), ())), preferred_element_type=F32)


def exchange_groups(blocks):
    count = len(blocks)
    group = LANES // count
    lane_group = lax.broadcasted_iota(jnp.int32, blocks[0].shape, 1) // group
    skewed = [blocks[0]] + [pltpu.roll(blocks[r], r * group, 1) for r in range(1, count)]
    result = []
    for p in range(count):
        value = skewed[0]
        for r in range(1, count):
            value = jnp.where(lane_group == (p + r) % count, skewed[r], value)
        if p > 0:
            value = pltpu.roll(value, LANES - p * group, 1)
        result.append(value)
    return result


def kernel(
    parts, bands, conv_at, grad_at, w_in_at, b_in_at, w_out_at, weight_at, filt_at, offsets_at, ana_at, syn_at,
    out,
    conv_n, grad_n, conv, grad, w_in, b_in, w_out, weight, filt, offsets, ana, syn, pre, slope, send, recv, spec, z_out, z_low, z_high, low, high,
    gain, flipped, wlines, outspec, ret_send, ret_recv,
    a_send, a_recv, z_send, z_recv, r_send, r_recv, loads,
):
    lon, rows, channels = conv_n.shape
    hidden = w_in.shape[1]
    tiles = channels // LANES
    group = LANES // rows
    pad = conv.shape[0] // rows
    me = lax.axis_index("azimuth")
    band = lax.axis_index("polar")
    bases, lat, modes2 = filt.shape
    modes = modes2 // 2
    width = rows + 2 * REACH
    rest = modes2 // rows
    body = modes2 - rest
    has_low = band > 0
    has_high = band < bands - 1

    far = lax.rem(me - lax.rem(me, 2) + 2, parts)
    peers = [far, far + 1, me + 1 - 2 * lax.rem(me, 2)]

    barrier = pltpu.get_barrier_semaphore()
    for peer in peers:
        pl.semaphore_signal(barrier, inc=1, device_id={"azimuth": peer}, device_id_type=MESH)

    @pl.when(has_low)
    def _():
        pl.semaphore_signal(barrier, inc=1, device_id={"polar": band - 1}, device_id_type=MESH)

    @pl.when(has_high)
    def _():
        pl.semaphore_signal(barrier, inc=1, device_id={"polar": band + 1}, device_id_type=MESH)

    piece = 2 * LANES
    loading = {}

    def load(name, src, dst):
        loading[name] = pltpu.make_async_copy(src, dst, loads.at[len(loading)])
        loading[name].start()

    pieces = hidden // piece
    load("conv", conv_at, conv_n)
    early = 2 * piece
    load("w_in", w_in_at.at[:, 0:early], w_in.at[:, 0:early])
    load("b_in", b_in_at, b_in)
    load("w_in_rest", w_in_at.at[:, early:], w_in.at[:, early:])

    @pl.when(jnp.logical_not(has_low))
    def _():
        z_low[...] = jnp.zeros(z_low.shape, BF16)

    @pl.when(jnp.logical_not(has_high))
    def _():
        z_high[...] = jnp.zeros(z_high.shape, BF16)

    def unweave(src, dst):
        turned = jnp.transpose(src[...], (1, 0, 2))
        for row in range(rows):
            dst[row * pad : row * pad + lon, :] = turned[row]
            dst[row * pad + lon : (row + 1) * pad, :] = jnp.zeros((pad - lon, channels), BF16)

    def columns(n):
        return slice(n * piece, (n + 1) * piece)

    def forward(n):
        pre[:, columns(n)] = dot(conv[...], w_in[:, columns(n)]) + b_in[columns(n)][None, :]

    def backward(n):
        back = dot_nt(grad[...], w_out[columns(n), :])
        slope[:, columns(n)] = (back * gelu_slope(pre[:, columns(n)])).astype(BF16)

    loading["conv"].wait()
    unweave(conv_n, conv)
    loading["w_in"].wait()
    load("grad", grad_at, grad_n)
    loading["b_in"].wait()
    ahead = 3
    for n in range(pieces + ahead):
        if n == 2:
            loading["w_in_rest"].wait()
        if n == 1:
            load("w_out", w_out_at, w_out)
        if n < pieces:
            forward(n)
        if n == ahead:
            loading["grad"].wait()
            unweave(grad_n, grad)
            loading["w_out"].wait()
            load("filt", filt_at, filt)
            load("offsets", offsets_at, offsets)
            load("weight", weight_at, weight)
            load("ana", ana_at, ana)
            load("syn", syn_at, syn)
        if n >= ahead:
            backward(n - ahead)

    neighbours = jnp.where(has_low, 1, 0) + jnp.where(has_high, 1, 0)
    pl.semaphore_wait(barrier, parts - 1 + neighbours)

    def a_copy(peer, k, src_at, dst_at):
        return pltpu.make_async_remote_copy(
            src_ref=send.at[src_at, k], dst_ref=recv.at[k, dst_at],
            send_sem=a_send.at[src_at, k], recv_sem=a_recv.at[dst_at, k],
            device_id={"azimuth": peer}, device_id_type=MESH,
        )

    def r_copy(peer, k, src_at, dst_at):
        return pltpu.make_async_remote_copy(
            src_ref=ret_send.at[src_at, k], dst_ref=ret_recv.at[k, dst_at],
            send_sem=r_send.at[src_at, k], recv_sem=r_recv.at[dst_at, k],
            device_id={"azimuth": peer}, device_id_type=MESH,
        )

    def up_copy(k):
        return pltpu.make_async_remote_copy(
            src_ref=z_out.at[0, k], dst_ref=z_low.at[k], send_sem=z_send.at[0, k], recv_sem=z_recv.at[0, k],
            device_id={"polar": band + 1}, device_id_type=MESH,
        )

    def down_copy(k):
        return pltpu.make_async_remote_copy(
            src_ref=z_out.at[1, k], dst_ref=z_high.at[k], send_sem=z_send.at[1, k], recv_sem=z_recv.at[1, k],
            device_id={"polar": band - 1}, device_id_type=MESH,
        )

    def hidden_tiles(begin, end):
        full = dot_nt(slope[...], w_in[begin * LANES : end * LANES, :])
        for k in range(begin, end):
            cols = slice((k - begin) * LANES, (k - begin + 1) * LANES)
            mixed = exchange_groups([full[row * pad : (row + 1) * pad, cols].astype(BF16) for row in range(rows)])
            for part in range(parts):
                send[part, k] = mixed[part][:lon]
            for peer in peers:
                a_copy(peer, k, peer, me).start()
            recv[k, me] = send[me, k]

    hidden_tiles(0, 1)
    for begin in range(1, tiles, 2):
        hidden_tiles(begin, min(begin + 2, tiles))
    def lane_groups(size):
        return lax.broadcasted_iota(jnp.int32, (size, LANES), 1) // group

    def analyze(k):
        if k == 0:
            loading["ana"].wait()
        for peer in peers:
            a_copy(peer, k, peer, peer).wait_recv()
        total = dot(ana[0], recv[k, 0])
        for src in range(1, parts):
            total = total + dot(ana[src], recv[k, src])
        spec[k] = total.astype(BF16)
        main, extra = total[:body], total[body:]
        free = lane_groups(rest)
        for g in range(REACH):
            at = slice(g * rest, (g + 1) * rest)
            moved = pltpu.roll(extra, LANES - (g + 1) * group, 1)
            z_out[0, k, at, :] = jnp.where(free == 0, moved, main[at]).astype(BF16)
        for g in range(REACH):
            at = slice(g * rest, (g + 1) * rest)
            moved = pltpu.roll(extra, (REACH - g) * group, 1)
            z_out[1, k, at, :] = jnp.where(free == REACH, moved, main[at]).astype(BF16)

        @pl.when(has_high)
        def _():
            up_copy(k).start()

        @pl.when(has_low)
        def _():
            down_copy(k).start()

    analyze(0)
    for name in ("filt", "offsets", "weight"):
        loading[name].wait()

    half = bases * width
    lines = 2 * half

    def line_parts(lanes):
        line = lax.broadcasted_iota(jnp.int32, (lines, lanes), 0)
        low_bits = line >= half
        line = jnp.where(low_bits, line - half, line)
        basis = line // width
        return low_bits, basis, line - basis * width, lax.broadcasted_iota(jnp.int32, (lines, lanes), 1)

    start_lat = band * rows - REACH
    low_bits, basis, place, lane = line_parts(bases * lat)
    pick = jnp.where(lane == basis * lat + place + start_lat, 1.0, 0.0)
    pick = jnp.where((place + start_lat >= 0) & (place + start_lat < lat), pick, 0.0)
    f_t = dot(pick.astype(BF16), filt[...].reshape(bases * lat, modes2))
    flipped[...] = jnp.transpose(f_t).astype(BF16)
    low_bits, basis, place, lane = line_parts(lat)
    pick = jnp.where(lane == place + start_lat, 1.0, 0.0).astype(BF16)
    rows_of = dot(pick, offsets[...].astype(F32).astype(BF16))
    low_bits, basis, place, lane = line_parts(bases)
    goal = jnp.sum(jnp.where(lane == basis, rows_of, 0.0), axis=1, keepdims=True)
    goal = jnp.broadcast_to(goal.astype(jnp.int32) - band * rows, (lines, LANES))
    mine = []
    for k in range(tiles):
        tile = weight[:, k * LANES : (k + 1) * LANES]
        chosen = jnp.concatenate([tile[:, 0:group]] * rows, axis=1)
        for part in range(1, parts):
            spread = jnp.concatenate([tile[:, part * group : (part + 1) * group]] * rows, axis=1)
            chosen = jnp.where(me == part, spread, chosen)
        mine.append(chosen)
    weights = jnp.concatenate(mine, axis=1)
    top = weights.astype(BF16)
    remainder = (weights - top.astype(F32)).astype(BF16)
    chosen = jnp.where(lane == basis, 1.0, 0.0)
    wlines[...] = dot(jnp.where(low_bits, 0.0, chosen).astype(BF16), top) + dot(
        jnp.where(low_bits, chosen, 0.0).astype(BF16), remainder
    )
    low_bits, basis, source, lane = line_parts(LANES)
    lane_row = lane // group

    def aimed(shift):
        target = lax.rem(lane_row + 2 * rows - (shift - REACH), rows)
        return (goal == target) & (source == target + shift)

    def make_gain(k):
        scale = wlines[:, k * LANES : (k + 1) * LANES]
        table = jnp.concatenate(
            [jnp.where(aimed(shift), scale, 0.0).astype(BF16) for shift in range(SHIFTS)], axis=1
        )
        made = dot(flipped[...], table)
        for shift in range(SHIFTS):
            gain[k * SHIFTS + shift] = made[:, shift * LANES : (shift + 1) * LANES]

    chunk = 64

    def filter_tile(k):
        if k == 0:
            loading["syn"].wait()

        @pl.when(has_low)
        def _():
            up_copy(k).wait_recv()

        @pl.when(has_high)
        def _():
            down_copy(k).wait_recv()

        free = lane_groups(rest)
        low[0:body, :] = z_low[k]
        high[0:body, :] = z_high[k]
        tail_low = jnp.zeros((rest, LANES), F32)
        tail_high = jnp.zeros((rest, LANES), F32)
        for g in range(REACH):
            at = slice(g * rest, (g + 1) * rest)
            moved = pltpu.roll(z_low[k, at, :].astype(F32), (g + 1) * group, 1)
            tail_low = jnp.where(free == g + 1, moved, tail_low)
            moved = pltpu.roll(z_high[k, at, :].astype(F32), LANES - (REACH - g) * group, 1)
            tail_high = jnp.where(free == g, moved, tail_high)
        low[body:, :] = tail_low.astype(BF16)
        high[body:, :] = tail_high.astype(BF16)
        lane_group = lane_groups(chunk)

        def one(it, carry):
            re = pl.ds(it * chunk, chunk)
            im = pl.ds(modes + it * chunk, chunk)

            def product(shift, sr, si):
                gr, gi = gain[k * SHIFTS + shift, re, :], gain[k * SHIFTS + shift, im, :]
                return gr * sr + gi * si, gr * si - gi * sr

            low_r, own_r, high_r = (ref[re, :].astype(F32) for ref in (low, spec.at[k], high))
            low_i, own_i, high_i = (ref[im, :].astype(F32) for ref in (low, spec.at[k], high))
            real, imag = product(REACH, own_r, own_i)
            for turn in range(1, rows):
                kept = lane_group >= turn
                up_r, up_i = product(
                    REACH + turn, jnp.where(kept, own_r, high_r), jnp.where(kept, own_i, high_i)
                )
                down_r, down_i = product(
                    REACH + turn - rows, jnp.where(kept, low_r, own_r), jnp.where(kept, low_i, own_i)
                )
                real = real + pltpu.roll(up_r + down_r, LANES - turn * group, 1)
                imag = imag + pltpu.roll(up_i + down_i, LANES - turn * group, 1)
            outspec[re, :] = real.astype(BF16)
            outspec[im, :] = imag.astype(BF16)
            return carry

        lax.fori_loop(0, modes // chunk, one, 0, unroll=True)
        near = me - lax.rem(me, 2)
        for first in (far, near):
            full = dot(syn[pl.ds(pl.multiple_of(first * pad, pad), 2 * pad), :], outspec[...])
            for part in range(2):
                ret_send[first + part, k] = full[part * pad : part * pad + lon].astype(BF16)
            for peer in peers[:2] if first is far else peers[2:]:
                r_copy(peer, k, peer, me).start()
        ret_recv[k, me] = ret_send[me, k]

    def finish(k):
        for peer in peers:
            r_copy(peer, k, peer, peer).wait_recv()
        sums = exchange_groups([ret_recv[k, src] for src in range(parts)])
        cols = slice(k * LANES, (k + 1) * LANES)
        done = [
            (sums[row].astype(F32) + grad[row * pad : row * pad + lon, cols].astype(F32)).astype(BF16) for row in range(rows)
        ]
        out[:, :, cols] = jnp.transpose(jnp.stack(done, axis=0), (1, 0, 2))

    order = (
        [("g", 0), ("a", 1), ("g", 1), ("g", 2), ("a", 2), ("g", 3), ("g", 4), ("f", 0), ("a", 3), ("f", 1)]
        + [("a", 4), ("f", 2), ("e", 0), ("f", 3), ("e", 1), ("f", 4), ("e", 2), ("e", 3), ("e", 4)]
    )
    if tiles != 5:
        order = [(what, k) for what in "gafe" for k in range(tiles) if (what, k) != ("a", 0)]
    for what, k in order:
        {"g": make_gain, "a": analyze, "f": filter_tile, "e": finish}[what](k)

    for k in range(tiles):
        for peer in peers:
            a_copy(peer, k, peer, me).wait_send()
            r_copy(peer, k, peer, me).wait_send()

        @pl.when(has_high)
        def _():
            up_copy(k).wait_send()

        @pl.when(has_low)
        def _():
            down_copy(k).wait_send()


def on_device(parts, bands, conv_out, grad_out, w_in, b_in, w_out, basis_weight, filt, offsets):
    rows, lon, channels = conv_out.shape
    hidden = w_in.shape[1]
    assert parts == rows == REACH + 1 and LANES % parts == 0 and channels % LANES == 0
    modes2 = filt.shape[2]
    modes = modes2 // 2
    bases, width = filt.shape[0], rows + 2 * REACH
    assert filt.shape[1] <= 256 and modes2 % (16 * rows) == 0 and hidden % (2 * LANES) == 0
    analysis, synth = fourier_tables(parts * lon, modes)
    ana = np.ascontiguousarray(
        analysis.reshape(parts, lon, modes2).transpose(0, 2, 1)
    ).astype(ml_dtypes.bfloat16)
    tiles = channels // LANES
    pad = -(-lon // 16) * 16
    syn = np.zeros((parts, pad, modes2), ml_dtypes.bfloat16)
    syn[:, :lon] = synth.reshape(parts, lon, modes2)
    syn = syn.reshape(parts * pad, modes2)
    body = modes2 - modes2 // rows
    vmem = pl.BlockSpec(memory_space=pltpu.VMEM)
    hbm = pl.BlockSpec(memory_space=pl.ANY)
    dma = pltpu.SemaphoreType.DMA
    result = pl.pallas_call(
        functools.partial(kernel, parts, bands),
        out_shape=pltpu.VMEM((lon, rows, channels), BF16),
        in_specs=[hbm] * 10,
        out_specs=vmem,
        scratch_shapes=[
            pltpu.VMEM((lon, rows, channels), BF16),
            pltpu.VMEM((lon, rows, channels), BF16),
            pltpu.VMEM((rows * pad, channels), BF16),
            pltpu.VMEM((rows * pad, channels), BF16),
            pltpu.VMEM(w_in.shape, BF16),
            pltpu.VMEM(b_in.shape, F32),
            pltpu.VMEM(w_out.shape, BF16),
            pltpu.VMEM(basis_weight.shape, F32),
            pltpu.VMEM(filt.shape, BF16),
            pltpu.VMEM(offsets.shape, jnp.int32),
            pltpu.VMEM(ana.shape, BF16),
            pltpu.VMEM(syn.shape, BF16),
            pltpu.VMEM((rows * pad, hidden), F32),
            pltpu.VMEM((rows * pad, hidden), BF16),
            pltpu.VMEM((parts, tiles, lon, LANES), BF16),
            pltpu.VMEM((tiles, parts, lon, LANES), BF16),
            pltpu.VMEM((tiles, modes2, LANES), BF16),
            pltpu.VMEM((2, tiles, body, LANES), BF16),
            pltpu.VMEM((tiles, body, LANES), BF16),
            pltpu.VMEM((tiles, body, LANES), BF16),
            pltpu.VMEM((modes2, LANES), BF16),
            pltpu.VMEM((modes2, LANES), BF16),
            pltpu.VMEM((tiles * SHIFTS, modes2, LANES), F32),
            pltpu.VMEM((modes2, 2 * bases * width), BF16),
            pltpu.VMEM((2 * bases * width, channels), F32),
            pltpu.VMEM((modes2, LANES), BF16),
            pltpu.VMEM((parts, tiles, lon, LANES), BF16),
            pltpu.VMEM((tiles, parts, lon, LANES), BF16),
            dma((parts, tiles)),
            dma((parts, tiles)),
            dma((2, tiles)),
            dma((2, tiles)),
            dma((parts, tiles)),
            dma((parts, tiles)),
            dma((11,)),
        ],
        compiler_params=pltpu.CompilerParams(
            collective_id=0, has_side_effects=True, vmem_limit_bytes=56 * 1024 * 1024
        ),
    )(jnp.transpose(conv_out, (1, 0, 2)), jnp.transpose(grad_out, (1, 0, 2)), w_in, b_in, w_out, basis_weight, filt, offsets,
      jnp.asarray(ana), jnp.asarray(syn))
    return jnp.transpose(result, (1, 0, 2))


def solution(mesh):
    grid = P(("member", "polar"), "azimuth", None)
    return jax.shard_map(
        functools.partial(on_device, mesh.shape["azimuth"], mesh.shape["polar"]),
        mesh=mesh,
        in_specs=(grid, grid, P(), P(), P(), P(), P(), P()),
        out_specs=grid,
        check_vma=False,
    )
```

```python
import functools
import math

import jax
import jax.numpy as jnp
import ml_dtypes
import numpy as np
from jax import lax
from jax.experimental import pallas as pl
from jax.experimental.pallas import tpu as pltpu
from jax.sharding import PartitionSpec as P

REACH = 3
LANES = 128
SHIFTS = 2 * REACH + 1
MESH = pl.DeviceIdType.MESH
F32 = jnp.float32
BF16 = jnp.bfloat16


def fourier_tables(length, modes):
    phase = np.arange(length)[:, None] * np.arange(modes)[None, :] % length
    angle = 2.0 * math.pi / length * phase
    scale = 1.0 / math.sqrt(length)
    factor = np.where(np.arange(modes) == 0, 1.0, 2.0)[None, :]
    analysis = np.concatenate([np.cos(angle), -np.sin(angle)], axis=1) * scale
    synth = np.concatenate([np.cos(angle) * factor, -np.sin(angle) * factor], axis=1) * scale
    return analysis, synth


def gelu_slope(values):
    normal_cdf = 0.5 * (1.0 + lax.erf(values * (1.0 / math.sqrt(2.0))))
    density = jnp.exp(-0.5 * values * values) * (1.0 / math.sqrt(2.0 * math.pi))
    return normal_cdf + values * density


def dot(a, b):
    return jnp.dot(a, b, preferred_element_type=F32)


def dot_nt(a, b):
    return lax.dot_general(a, b, (((1,), (1,)), ((), ())), preferred_element_type=F32)


def exchange_groups(blocks):
    count = len(blocks)
    group = LANES // count
    lane_group = lax.broadcasted_iota(jnp.int32, blocks[0].shape, 1) // group
    skewed = [blocks[0]] + [pltpu.roll(blocks[r], r * group, 1) for r in range(1, count)]
    result = []
    for p in range(count):
        value = skewed[0]
        for r in range(1, count):
            value = jnp.where(lane_group == (p + r) % count, skewed[r], value)
        if p > 0:
            value = pltpu.roll(value, LANES - p * group, 1)
        result.append(value)
    return result


def kernel(
    parts, bands, conv_at, grad_at, w_in_at, b_in_at, w_out_at, weight_at, filt_at, offsets_at, ana_at, syn_at,
    out,
    conv_n, grad_n, conv, grad, w_in, b_in, w_out, weight, filt, offsets, ana, syn, pre, first_tile, slope, send, recv, spec, z_out, z_low, z_high, low, high,
    gain, flipped, wlines, outspec, ret_send, ret_recv,
    a_send, a_recv, z_send, z_recv, r_send, r_recv, loads,
):
    lon, rows, channels = conv_n.shape
    hidden = w_in.shape[1]
    tiles = channels // LANES
    group = LANES // rows
    pad = conv.shape[0] // rows
    me = lax.axis_index("azimuth")
    band = lax.axis_index("polar")
    bases, lat, modes2 = filt.shape
    modes = modes2 // 2
    width = rows + 2 * REACH
    rest = modes2 // rows
    body = modes2 - rest
    has_low = band > 0
    has_high = band < bands - 1

    far = lax.rem(me - lax.rem(me, 2) + 2, parts)
    peers = [far, far + 1, me + 1 - 2 * lax.rem(me, 2)]

    barrier = pltpu.get_barrier_semaphore()
    for peer in peers:
        pl.semaphore_signal(barrier, inc=1, device_id={"azimuth": peer}, device_id_type=MESH)

    @pl.when(has_low)
    def _():
        pl.semaphore_signal(barrier, inc=1, device_id={"polar": band - 1}, device_id_type=MESH)

    @pl.when(has_high)
    def _():
        pl.semaphore_signal(barrier, inc=1, device_id={"polar": band + 1}, device_id_type=MESH)

    piece = 2 * LANES
    loading = {}

    def load(name, src, dst):
        loading[name] = pltpu.make_async_copy(src, dst, loads.at[len(loading)])
        loading[name].start()

    pieces = hidden // piece
    load("conv", conv_at, conv_n)
    early = 2 * piece
    load("w_in", w_in_at.at[:, 0:early], w_in.at[:, 0:early])
    load("b_in", b_in_at, b_in)
    load("w_in_rest", w_in_at.at[:, early:], w_in.at[:, early:])

    @pl.when(jnp.logical_not(has_low))
    def _():
        z_low[...] = jnp.zeros(z_low.shape, BF16)

    @pl.when(jnp.logical_not(has_high))
    def _():
        z_high[...] = jnp.zeros(z_high.shape, BF16)

    def unweave(src, dst):
        turned = jnp.transpose(src[...], (1, 0, 2))
        for row in range(rows):
            dst[row * pad : row * pad + lon, :] = turned[row]
            dst[row * pad + lon : (row + 1) * pad, :] = jnp.zeros((pad - lon, channels), BF16)

    def columns(n):
        return slice(n * piece, (n + 1) * piece)

    def forward(n):
        pre[:, columns(n)] = dot(conv[...], w_in[:, columns(n)]) + b_in[columns(n)][None, :]

    def backward(n):
        back = dot_nt(grad[...], w_out[columns(n), :])
        part = (back * gelu_slope(pre[:, columns(n)])).astype(BF16)
        slope[:, columns(n)] = part
        early_sum = dot_nt(part, w_in[0:LANES, columns(n)])
        first_tile[...] = early_sum if n == 0 else first_tile[...] + early_sum

    loading["conv"].wait()
    unweave(conv_n, conv)
    loading["w_in"].wait()
    load("grad", grad_at, grad_n)
    loading["b_in"].wait()
    ahead = 3
    for n in range(pieces + ahead):
        if n == 2:
            loading["w_in_rest"].wait()
        if n == 1:
            load("w_out", w_out_at, w_out)
        if n < pieces:
            forward(n)
        if n == ahead:
            loading["grad"].wait()
            unweave(grad_n, grad)
            loading["w_out"].wait()
            load("filt", filt_at, filt)
            load("offsets", offsets_at, offsets)
            load("weight", weight_at, weight)
            load("ana", ana_at, ana)
            load("syn", syn_at, syn)
        if n >= ahead:
            backward(n - ahead)

    neighbours = jnp.where(has_low, 1, 0) + jnp.where(has_high, 1, 0)
    pl.semaphore_wait(barrier, parts - 1 + neighbours)

    def a_copy(peer, k, src_at, dst_at):
        return pltpu.make_async_remote_copy(
            src_ref=send.at[src_at, k], dst_ref=recv.at[k, dst_at],
            send_sem=a_send.at[src_at, k], recv_sem=a_recv.at[dst_at, k],
            device_id={"azimuth": peer}, device_id_type=MESH,
        )

    def r_copy(peer, k, src_at, dst_at):
        return pltpu.make_async_remote_copy(
            src_ref=ret_send.at[src_at, k], dst_ref=ret_recv.at[k, dst_at],
            send_sem=r_send.at[src_at, k], recv_sem=r_recv.at[dst_at, k],
            device_id={"azimuth": peer}, device_id_type=MESH,
        )

    def up_copy(k):
        return pltpu.make_async_remote_copy(
            src_ref=z_out.at[0, k], dst_ref=z_low.at[k], send_sem=z_send.at[0, k], recv_sem=z_recv.at[0, k],
            device_id={"polar": band + 1}, device_id_type=MESH,
        )

    def down_copy(k):
        return pltpu.make_async_remote_copy(
            src_ref=z_out.at[1, k], dst_ref=z_high.at[k], send_sem=z_send.at[1, k], recv_sem=z_recv.at[1, k],
            device_id={"polar": band - 1}, device_id_type=MESH,
        )

    def hidden_tiles(begin, end):
        full = first_tile[...] if end == 1 else dot_nt(slope[...], w_in[begin * LANES : end * LANES, :])
        for k in range(begin, end):
            cols = slice((k - begin) * LANES, (k - begin + 1) * LANES)
            mixed = exchange_groups([full[row * pad : (row + 1) * pad, cols].astype(BF16) for row in range(rows)])
            for part in range(parts):
                send[part, k] = mixed[part][:lon]
            for peer in peers:
                a_copy(peer, k, peer, me).start()
            recv[k, me] = send[me, k]

    hidden_tiles(0, 1)
    for begin in range(1, tiles, 2):
        hidden_tiles(begin, min(begin + 2, tiles))
    def lane_groups(size):
        return lax.broadcasted_iota(jnp.int32, (size, LANES), 1) // group

    def analyze(k):
        if k == 0:
            loading["ana"].wait()
        total = dot(ana[me], recv[k, me])
        for peer in (peers[2], peers[0], peers[1]):
            a_copy(peer, k, peer, peer).wait_recv()
            total = total + dot(ana[peer], recv[k, peer])
        main, extra = total[:body], total[body:]
        free = lane_groups(rest)
        for g in range(REACH):
            at = slice(g * rest, (g + 1) * rest)
            moved = pltpu.roll(extra, LANES - (g + 1) * group, 1)
            z_out[0, k, at, :] = jnp.where(free == 0, moved, main[at]).astype(BF16)
        @pl.when(has_high)
        def _():
            up_copy(k).start()

        for g in range(REACH):
            at = slice(g * rest, (g + 1) * rest)
            moved = pltpu.roll(extra, (REACH - g) * group, 1)
            z_out[1, k, at, :] = jnp.where(free == REACH, moved, main[at]).astype(BF16)

        @pl.when(has_low)
        def _():
            down_copy(k).start()

        spec[k] = total.astype(BF16)

    analyze(0)
    for name in ("filt", "offsets", "weight"):
        loading[name].wait()

    half = bases * width
    lines = 2 * half

    def line_parts(lanes):
        line = lax.broadcasted_iota(jnp.int32, (lines, lanes), 0)
        low_bits = line >= half
        line = jnp.where(low_bits, line - half, line)
        basis = line // width
        return low_bits, basis, line - basis * width, lax.broadcasted_iota(jnp.int32, (lines, lanes), 1)

    start_lat = band * rows - REACH
    low_bits, basis, place, lane = line_parts(bases * lat)
    pick = jnp.where(lane == basis * lat + place + start_lat, 1.0, 0.0)
    pick = jnp.where((place + start_lat >= 0) & (place + start_lat < lat), pick, 0.0)
    f_t = dot(pick.astype(BF16), filt[...].reshape(bases * lat, modes2))
    flipped[...] = jnp.transpose(f_t).astype(BF16)
    low_bits, basis, place, lane = line_parts(lat)
    pick = jnp.where(lane == place + start_lat, 1.0, 0.0).astype(BF16)
    rows_of = dot(pick, offsets[...].astype(F32).astype(BF16))
    low_bits, basis, place, lane = line_parts(bases)
    goal = jnp.sum(jnp.where(lane == basis, rows_of, 0.0), axis=1, keepdims=True)
    goal = jnp.broadcast_to(goal.astype(jnp.int32) - band * rows, (lines, LANES))
    mine = []
    for k in range(tiles):
        tile = weight[:, k * LANES : (k + 1) * LANES]
        chosen = jnp.concatenate([tile[:, 0:group]] * rows, axis=1)
        for part in range(1, parts):
            spread = jnp.concatenate([tile[:, part * group : (part + 1) * group]] * rows, axis=1)
            chosen = jnp.where(me == part, spread, chosen)
        mine.append(chosen)
    weights = jnp.concatenate(mine, axis=1)
    top = weights.astype(BF16)
    remainder = (weights - top.astype(F32)).astype(BF16)
    chosen = jnp.where(lane == basis, 1.0, 0.0)
    wlines[...] = dot(jnp.where(low_bits, 0.0, chosen).astype(BF16), top) + dot(
        jnp.where(low_bits, chosen, 0.0).astype(BF16), remainder
    )
    low_bits, basis, source, lane = line_parts(LANES)
    lane_row = lane // group

    def aimed(shift):
        target = lax.rem(lane_row + 2 * rows - (shift - REACH), rows)
        return (goal == target) & (source == target + shift)

    def make_gain(k):
        scale = wlines[:, k * LANES : (k + 1) * LANES]
        table = jnp.concatenate(
            [jnp.where(aimed(shift), scale, 0.0).astype(BF16) for shift in range(SHIFTS)], axis=1
        )
        made = dot(flipped[...], table)
        for shift in range(SHIFTS):
            gain[k * SHIFTS + shift] = made[:, shift * LANES : (shift + 1) * LANES]

    chunk = 64

    def filter_tile(k):
        if k == 0:
            loading["syn"].wait()

        @pl.when(has_low)
        def _():
            up_copy(k).wait_recv()

        @pl.when(has_high)
        def _():
            down_copy(k).wait_recv()

        free = lane_groups(rest)
        low[0:body, :] = z_low[k]
        high[0:body, :] = z_high[k]
        tail_low = jnp.zeros((rest, LANES), F32)
        tail_high = jnp.zeros((rest, LANES), F32)
        for g in range(REACH):
            at = slice(g * rest, (g + 1) * rest)
            moved = pltpu.roll(z_low[k, at, :].astype(F32), (g + 1) * group, 1)
            tail_low = jnp.where(free == g + 1, moved, tail_low)
            moved = pltpu.roll(z_high[k, at, :].astype(F32), LANES - (REACH - g) * group, 1)
            tail_high = jnp.where(free == g, moved, tail_high)
        low[body:, :] = tail_low.astype(BF16)
        high[body:, :] = tail_high.astype(BF16)
        lane_group = lane_groups(chunk)

        def one(it, carry):
            re = pl.ds(it * chunk, chunk)
            im = pl.ds(modes + it * chunk, chunk)

            def product(shift, sr, si):
                gr, gi = gain[k * SHIFTS + shift, re, :], gain[k * SHIFTS + shift, im, :]
                return gr * sr + gi * si, gr * si - gi * sr

            low_r, own_r, high_r = (ref[re, :].astype(F32) for ref in (low, spec.at[k], high))
            low_i, own_i, high_i = (ref[im, :].astype(F32) for ref in (low, spec.at[k], high))
            real, imag = product(REACH, own_r, own_i)
            for turn in range(1, rows):
                kept = lane_group >= turn
                up_r, up_i = product(
                    REACH + turn, jnp.where(kept, own_r, high_r), jnp.where(kept, own_i, high_i)
                )
                down_r, down_i = product(
                    REACH + turn - rows, jnp.where(kept, low_r, own_r), jnp.where(kept, low_i, own_i)
                )
                real = real + pltpu.roll(up_r + down_r, LANES - turn * group, 1)
                imag = imag + pltpu.roll(up_i + down_i, LANES - turn * group, 1)
            outspec[re, :] = real.astype(BF16)
            outspec[im, :] = imag.astype(BF16)
            return carry

        lax.fori_loop(0, modes // chunk, one, 0, unroll=True)
        near = me - lax.rem(me, 2)
        for first in (far, near):
            full = dot(syn[pl.ds(pl.multiple_of(first * pad, pad), 2 * pad), :], outspec[...])
            for part in range(2):
                ret_send[first + part, k] = full[part * pad : part * pad + lon].astype(BF16)
            for peer in peers[:2] if first is far else peers[2:]:
                r_copy(peer, k, peer, me).start()
        ret_recv[k, me] = ret_send[me, k]

    def finish(k):
        for peer in peers:
            r_copy(peer, k, peer, peer).wait_recv()
        sums = exchange_groups([ret_recv[k, src] for src in range(parts)])
        cols = slice(k * LANES, (k + 1) * LANES)
        done = [
            (sums[row].astype(F32) + grad[row * pad : row * pad + lon, cols].astype(F32)).astype(BF16) for row in range(rows)
        ]
        out[:, :, cols] = jnp.transpose(jnp.stack(done, axis=0), (1, 0, 2))

    order = (
        [("g", 0), ("a", 1), ("g", 1), ("g", 2), ("a", 2), ("g", 3), ("g", 4), ("f", 0), ("a", 3), ("f", 1)]
        + [("a", 4), ("f", 2), ("e", 0), ("f", 3), ("e", 1), ("f", 4), ("e", 2), ("e", 3), ("e", 4)]
    )
    if tiles != 5:
        order = [(what, k) for what in "gafe" for k in range(tiles) if (what, k) != ("a", 0)]
    for what, k in order:
        {"g": make_gain, "a": analyze, "f": filter_tile, "e": finish}[what](k)

    for k in range(tiles):
        for peer in peers:
            a_copy(peer, k, peer, me).wait_send()
            r_copy(peer, k, peer, me).wait_send()

        @pl.when(has_high)
        def _():
            up_copy(k).wait_send()

        @pl.when(has_low)
        def _():
            down_copy(k).wait_send()


def on_device(parts, bands, conv_out, grad_out, w_in, b_in, w_out, basis_weight, filt, offsets):
    rows, lon, channels = conv_out.shape
    hidden = w_in.shape[1]
    assert parts == rows == REACH + 1 and LANES % parts == 0 and channels % LANES == 0
    modes2 = filt.shape[2]
    modes = modes2 // 2
    bases, width = filt.shape[0], rows + 2 * REACH
    assert filt.shape[1] <= 256 and modes2 % (16 * rows) == 0 and hidden % (2 * LANES) == 0
    analysis, synth = fourier_tables(parts * lon, modes)
    ana = np.ascontiguousarray(
        analysis.reshape(parts, lon, modes2).transpose(0, 2, 1)
    ).astype(ml_dtypes.bfloat16)
    tiles = channels // LANES
    pad = -(-lon // 16) * 16
    syn = np.zeros((parts, pad, modes2), ml_dtypes.bfloat16)
    syn[:, :lon] = synth.reshape(parts, lon, modes2)
    syn = syn.reshape(parts * pad, modes2)
    body = modes2 - modes2 // rows
    vmem = pl.BlockSpec(memory_space=pltpu.VMEM)
    hbm = pl.BlockSpec(memory_space=pl.ANY)
    dma = pltpu.SemaphoreType.DMA
    result = pl.pallas_call(
        functools.partial(kernel, parts, bands),
        out_shape=pltpu.VMEM((lon, rows, channels), BF16),
        in_specs=[hbm] * 10,
        out_specs=vmem,
        scratch_shapes=[
            pltpu.VMEM((lon, rows, channels), BF16),
            pltpu.VMEM((lon, rows, channels), BF16),
            pltpu.VMEM((rows * pad, channels), BF16),
            pltpu.VMEM((rows * pad, channels), BF16),
            pltpu.VMEM(w_in.shape, BF16),
            pltpu.VMEM(b_in.shape, F32),
            pltpu.VMEM(w_out.shape, BF16),
            pltpu.VMEM(basis_weight.shape, F32),
            pltpu.VMEM(filt.shape, BF16),
            pltpu.VMEM(offsets.shape, jnp.int32),
            pltpu.VMEM(ana.shape, BF16),
            pltpu.VMEM(syn.shape, BF16),
            pltpu.VMEM((rows * pad, hidden), F32),
            pltpu.VMEM((rows * pad, LANES), F32),
            pltpu.VMEM((rows * pad, hidden), BF16),
            pltpu.VMEM((parts, tiles, lon, LANES), BF16),
            pltpu.VMEM((tiles, parts, lon, LANES), BF16),
            pltpu.VMEM((tiles, modes2, LANES), BF16),
            pltpu.VMEM((2, tiles, body, LANES), BF16),
            pltpu.VMEM((tiles, body, LANES), BF16),
            pltpu.VMEM((tiles, body, LANES), BF16),
            pltpu.VMEM((modes2, LANES), BF16),
            pltpu.VMEM((modes2, LANES), BF16),
            pltpu.VMEM((tiles * SHIFTS, modes2, LANES), F32),
            pltpu.VMEM((modes2, 2 * bases * width), BF16),
            pltpu.VMEM((2 * bases * width, channels), F32),
            pltpu.VMEM((modes2, LANES), BF16),
            pltpu.VMEM((parts, tiles, lon, LANES), BF16),
            pltpu.VMEM((tiles, parts, lon, LANES), BF16),
            dma((parts, tiles)),
            dma((parts, tiles)),
            dma((2, tiles)),
            dma((2, tiles)),
            dma((parts, tiles)),
            dma((parts, tiles)),
            dma((11,)),
        ],
        compiler_params=pltpu.CompilerParams(
            collective_id=0, has_side_effects=True, vmem_limit_bytes=56 * 1024 * 1024
        ),
    )(jnp.transpose(conv_out, (1, 0, 2)), jnp.transpose(grad_out, (1, 0, 2)), w_in, b_in, w_out, basis_weight, filt, offsets,
      jnp.asarray(ana), jnp.asarray(syn))
    return jnp.transpose(result, (1, 0, 2))


def solution(mesh):
    grid = P(("member", "polar"), "azimuth", None)
    return jax.shard_map(
        functools.partial(on_device, mesh.shape["azimuth"], mesh.shape["polar"]),
        mesh=mesh,
        in_specs=(grid, grid, P(), P(), P(), P(), P(), P()),
        out_specs=grid,
        check_vma=False,
    )
```

```python
import functools
import math

import jax
import jax.numpy as jnp
import ml_dtypes
import numpy as np
from jax import lax
from jax.experimental import pallas as pl
from jax.experimental.pallas import tpu as pltpu
from jax.sharding import PartitionSpec as P

REACH = 3
LANES = 128
SHIFTS = 2 * REACH + 1
MESH = pl.DeviceIdType.MESH
F32 = jnp.float32
BF16 = jnp.bfloat16


def fourier_tables(length, modes):
    phase = np.arange(length)[:, None] * np.arange(modes)[None, :] % length
    angle = 2.0 * math.pi / length * phase
    scale = 1.0 / math.sqrt(length)
    factor = np.where(np.arange(modes) == 0, 1.0, 2.0)[None, :]
    analysis = np.concatenate([np.cos(angle), -np.sin(angle)], axis=1) * scale
    synth = np.concatenate([np.cos(angle) * factor, -np.sin(angle) * factor], axis=1) * scale
    return analysis, synth


def gelu_slope(values):
    normal_cdf = 0.5 * (1.0 + lax.erf(values * (1.0 / math.sqrt(2.0))))
    density = jnp.exp(-0.5 * values * values) * (1.0 / math.sqrt(2.0 * math.pi))
    return normal_cdf + values * density


def dot(a, b):
    return jnp.dot(a, b, preferred_element_type=F32)


def dot_nt(a, b):
    return lax.dot_general(a, b, (((1,), (1,)), ((), ())), preferred_element_type=F32)


def exchange_groups(blocks):
    count = len(blocks)
    group = LANES // count
    lane_group = lax.broadcasted_iota(jnp.int32, blocks[0].shape, 1) // group
    skewed = [blocks[0]] + [pltpu.roll(blocks[r], r * group, 1) for r in range(1, count)]
    result = []
    for p in range(count):
        value = skewed[0]
        for r in range(1, count):
            value = jnp.where(lane_group == (p + r) % count, skewed[r], value)
        if p > 0:
            value = pltpu.roll(value, LANES - p * group, 1)
        result.append(value)
    return result


def kernel(
    parts, bands, conv_at, grad_at, w_in_at, b_in_at, w_out_at, weight_at, filt_at, offsets_at, ana_at, syn_at,
    out,
    conv_n, grad_n, conv, grad, w_in, b_in, w_out, weight, filt, offsets, ana, syn, pre, first_tile, slope, send, recv, spec, z_out, z_low, z_high, low, high,
    gain, flipped, wlines, outspec, ret_send, ret_recv,
    a_send, a_recv, z_send, z_recv, r_send, r_recv, loads,
):
    lon, rows, channels = conv_n.shape
    hidden = w_in.shape[1]
    tiles = channels // LANES
    group = LANES // rows
    pad = conv.shape[0] // rows
    me = lax.axis_index("azimuth")
    band = lax.axis_index("polar")
    bases, lat, modes2 = filt.shape
    modes = modes2 // 2
    width = rows + 2 * REACH
    rest = modes2 // rows
    body = modes2 - rest
    has_low = band > 0
    has_high = band < bands - 1

    far = lax.rem(me - lax.rem(me, 2) + 2, parts)
    peers = [far, far + 1, me + 1 - 2 * lax.rem(me, 2)]

    barrier = pltpu.get_barrier_semaphore()
    for peer in peers:
        pl.semaphore_signal(barrier, inc=1, device_id={"azimuth": peer}, device_id_type=MESH)

    @pl.when(has_low)
    def _():
        pl.semaphore_signal(barrier, inc=1, device_id={"polar": band - 1}, device_id_type=MESH)

    @pl.when(has_high)
    def _():
        pl.semaphore_signal(barrier, inc=1, device_id={"polar": band + 1}, device_id_type=MESH)

    piece = 2 * LANES
    loading = {}

    def load(name, src, dst):
        loading[name] = pltpu.make_async_copy(src, dst, loads.at[len(loading)])
        loading[name].start()

    pieces = hidden // piece
    load("conv", conv_at, conv_n)
    early = 2 * piece
    load("w_in", w_in_at.at[:, 0:early], w_in.at[:, 0:early])
    load("b_in", b_in_at, b_in)
    load("w_in_rest", w_in_at.at[:, early:], w_in.at[:, early:])

    @pl.when(jnp.logical_not(has_low))
    def _():
        z_low[...] = jnp.zeros(z_low.shape, BF16)

    @pl.when(jnp.logical_not(has_high))
    def _():
        z_high[...] = jnp.zeros(z_high.shape, BF16)

    def unweave(src, dst):
        turned = jnp.transpose(src[...], (1, 0, 2))
        for row in range(rows):
            dst[row * pad : row * pad + lon, :] = turned[row]
            dst[row * pad + lon : (row + 1) * pad, :] = jnp.zeros((pad - lon, channels), BF16)

    def columns(n):
        return slice(n * piece, (n + 1) * piece)

    def forward(n):
        pre[:, columns(n)] = dot(conv[...], w_in[:, columns(n)]) + b_in[columns(n)][None, :]

    def backward(n):
        back = dot_nt(grad[...], w_out[columns(n), :])
        part = (back * gelu_slope(pre[:, columns(n)])).astype(BF16)
        slope[:, columns(n)] = part
        early_sum = dot_nt(part, w_in[0:LANES, columns(n)])
        first_tile[...] = early_sum if n == 0 else first_tile[...] + early_sum

    loading["conv"].wait()
    unweave(conv_n, conv)
    loading["w_in"].wait()
    load("grad", grad_at, grad_n)
    loading["b_in"].wait()
    ahead = 3
    for n in range(pieces + ahead):
        if n == 2:
            loading["w_in_rest"].wait()
        if n == 1:
            load("w_out", w_out_at, w_out)
        if n < pieces:
            forward(n)
        if n == ahead:
            loading["grad"].wait()
            unweave(grad_n, grad)
            loading["w_out"].wait()
            load("filt", filt_at, filt)
            load("offsets", offsets_at, offsets)
            load("weight", weight_at, weight)
            load("ana", ana_at, ana)
            load("syn", syn_at, syn)
        if n >= ahead:
            backward(n - ahead)

    neighbours = jnp.where(has_low, 1, 0) + jnp.where(has_high, 1, 0)
    pl.semaphore_wait(barrier, parts - 1 + neighbours)

    def a_copy(peer, k, src_at, dst_at):
        return pltpu.make_async_remote_copy(
            src_ref=send.at[src_at, k], dst_ref=recv.at[k, dst_at],
            send_sem=a_send.at[src_at, k], recv_sem=a_recv.at[dst_at, k],
            device_id={"azimuth": peer}, device_id_type=MESH,
        )

    def r_copy(peer, k, src_at, dst_at):
        return pltpu.make_async_remote_copy(
            src_ref=ret_send.at[src_at, k], dst_ref=ret_recv.at[k, dst_at],
            send_sem=r_send.at[src_at, k], recv_sem=r_recv.at[dst_at, k],
            device_id={"azimuth": peer}, device_id_type=MESH,
        )

    def up_copy(k):
        return pltpu.make_async_remote_copy(
            src_ref=z_out.at[0, k], dst_ref=z_low.at[k], send_sem=z_send.at[0, k], recv_sem=z_recv.at[0, k],
            device_id={"polar": band + 1}, device_id_type=MESH,
        )

    def down_copy(k):
        return pltpu.make_async_remote_copy(
            src_ref=z_out.at[1, k], dst_ref=z_high.at[k], send_sem=z_send.at[1, k], recv_sem=z_recv.at[1, k],
            device_id={"polar": band - 1}, device_id_type=MESH,
        )

    def hidden_tiles(begin, end):
        full = first_tile[...] if end == 1 else dot_nt(slope[...], w_in[begin * LANES : end * LANES, :])
        for k in range(begin, end):
            cols = slice((k - begin) * LANES, (k - begin + 1) * LANES)
            mixed = exchange_groups([full[row * pad : (row + 1) * pad, cols].astype(BF16) for row in range(rows)])
            for part in range(parts):
                send[part, k] = mixed[part][:lon]
            for peer in peers:
                a_copy(peer, k, peer, me).start()
            recv[k, me] = send[me, k]

    hidden_tiles(0, 1)
    for begin in range(1, tiles, 2):
        hidden_tiles(begin, min(begin + 2, tiles))
    def lane_groups(size):
        return lax.broadcasted_iota(jnp.int32, (size, LANES), 1) // group

    def analyze(k):
        if k == 0:
            loading["ana"].wait()
        total = dot(ana[me], recv[k, me])
        for peer in (peers[2], peers[0], peers[1]):
            a_copy(peer, k, peer, peer).wait_recv()
            total = total + dot(ana[peer], recv[k, peer])
        main, extra = total[:body], total[body:]
        free = lane_groups(rest)
        for g in range(REACH):
            at = slice(g * rest, (g + 1) * rest)
            moved = pltpu.roll(extra, LANES - (g + 1) * group, 1)
            z_out[0, k, at, :] = jnp.where(free == 0, moved, main[at]).astype(BF16)
        @pl.when(has_high)
        def _():
            up_copy(k).start()

        for g in range(REACH):
            at = slice(g * rest, (g + 1) * rest)
            moved = pltpu.roll(extra, (REACH - g) * group, 1)
            z_out[1, k, at, :] = jnp.where(free == REACH, moved, main[at]).astype(BF16)

        @pl.when(has_low)
        def _():
            down_copy(k).start()

        spec[k] = total.astype(BF16)

    analyze(0)
    for name in ("filt", "offsets", "weight"):
        loading[name].wait()

    half = bases * width
    lines = 2 * half

    def line_parts(lanes):
        line = lax.broadcasted_iota(jnp.int32, (lines, lanes), 0)
        low_bits = line >= half
        line = jnp.where(low_bits, line - half, line)
        basis = line // width
        return low_bits, basis, line - basis * width, lax.broadcasted_iota(jnp.int32, (lines, lanes), 1)

    start_lat = band * rows - REACH
    low_bits, basis, place, lane = line_parts(bases * lat)
    pick = jnp.where(lane == basis * lat + place + start_lat, 1.0, 0.0)
    pick = jnp.where((place + start_lat >= 0) & (place + start_lat < lat), pick, 0.0)
    f_t = dot(pick.astype(BF16), filt[...].reshape(bases * lat, modes2))
    flipped[...] = jnp.transpose(f_t).astype(BF16)
    low_bits, basis, place, lane = line_parts(lat)
    pick = jnp.where(lane == place + start_lat, 1.0, 0.0).astype(BF16)
    rows_of = dot(pick, offsets[...].astype(F32).astype(BF16))
    low_bits, basis, place, lane = line_parts(bases)
    goal = jnp.sum(jnp.where(lane == basis, rows_of, 0.0), axis=1, keepdims=True)
    goal = jnp.broadcast_to(goal.astype(jnp.int32) - band * rows, (lines, LANES))
    mine = []
    for k in range(tiles):
        tile = weight[:, k * LANES : (k + 1) * LANES]
        chosen = jnp.concatenate([tile[:, 0:group]] * rows, axis=1)
        for part in range(1, parts):
            spread = jnp.concatenate([tile[:, part * group : (part + 1) * group]] * rows, axis=1)
            chosen = jnp.where(me == part, spread, chosen)
        mine.append(chosen)
    weights = jnp.concatenate(mine, axis=1)
    top = weights.astype(BF16)
    remainder = (weights - top.astype(F32)).astype(BF16)
    chosen = jnp.where(lane == basis, 1.0, 0.0)
    wlines[...] = dot(jnp.where(low_bits, 0.0, chosen).astype(BF16), top) + dot(
        jnp.where(low_bits, chosen, 0.0).astype(BF16), remainder
    )
    low_bits, basis, source, lane = line_parts(LANES)
    lane_row = lane // group

    def aimed(shift):
        target = lax.rem(lane_row + 2 * rows - (shift - REACH), rows)
        return (goal == target) & (source == target + shift)

    def make_gain(k):
        scale = wlines[:, k * LANES : (k + 1) * LANES]
        table = jnp.concatenate(
            [jnp.where(aimed(shift), scale, 0.0).astype(BF16) for shift in range(SHIFTS)], axis=1
        )
        made = dot(flipped[...], table)
        for shift in range(SHIFTS):
            gain[k * SHIFTS + shift] = made[:, shift * LANES : (shift + 1) * LANES]

    chunk = 64

    def filter_tile(k):
        if k == 0:
            loading["syn"].wait()

        @pl.when(has_low)
        def _():
            up_copy(k).wait_recv()

        @pl.when(has_high)
        def _():
            down_copy(k).wait_recv()

        free = lane_groups(rest)
        low[0:body, :] = z_low[k]
        high[0:body, :] = z_high[k]
        tail_low = jnp.zeros((rest, LANES), F32)
        tail_high = jnp.zeros((rest, LANES), F32)
        for g in range(REACH):
            at = slice(g * rest, (g + 1) * rest)
            moved = pltpu.roll(z_low[k, at, :].astype(F32), (g + 1) * group, 1)
            tail_low = jnp.where(free == g + 1, moved, tail_low)
            moved = pltpu.roll(z_high[k, at, :].astype(F32), LANES - (REACH - g) * group, 1)
            tail_high = jnp.where(free == g, moved, tail_high)
        low[body:, :] = tail_low.astype(BF16)
        high[body:, :] = tail_high.astype(BF16)
        lane_group = lane_groups(chunk)

        def one(it, carry):
            re = pl.ds(it * chunk, chunk)
            im = pl.ds(modes + it * chunk, chunk)

            def product(shift, sr, si):
                gr, gi = gain[k * SHIFTS + shift, re, :], gain[k * SHIFTS + shift, im, :]
                return gr * sr + gi * si, gr * si - gi * sr

            low_r, own_r, high_r = (ref[re, :].astype(F32) for ref in (low, spec.at[k], high))
            low_i, own_i, high_i = (ref[im, :].astype(F32) for ref in (low, spec.at[k], high))
            real, imag = product(REACH, own_r, own_i)
            for turn in range(1, rows):
                kept = lane_group >= turn
                up_r, up_i = product(
                    REACH + turn, jnp.where(kept, own_r, high_r), jnp.where(kept, own_i, high_i)
                )
                down_r, down_i = product(
                    REACH + turn - rows, jnp.where(kept, low_r, own_r), jnp.where(kept, low_i, own_i)
                )
                real = real + pltpu.roll(up_r + down_r, LANES - turn * group, 1)
                imag = imag + pltpu.roll(up_i + down_i, LANES - turn * group, 1)
            outspec[re, :] = real.astype(BF16)
            outspec[im, :] = imag.astype(BF16)
            return carry

        lax.fori_loop(0, modes // chunk, one, 0, unroll=True)
        near = me - lax.rem(me, 2)
        for first in (far, near):
            full = dot(syn[pl.ds(pl.multiple_of(first * pad, pad), 2 * pad), :], outspec[...])
            for part in range(2):
                ret_send[first + part, k] = full[part * pad : part * pad + lon].astype(BF16)
            for peer in peers[:2] if first is far else peers[2:]:
                r_copy(peer, k, peer, me).start()
        ret_recv[k, me] = ret_send[me, k]

    def finish(k):
        for peer in peers:
            r_copy(peer, k, peer, peer).wait_recv()
        sums = exchange_groups([ret_recv[k, src] for src in range(parts)])
        cols = slice(k * LANES, (k + 1) * LANES)
        done = [
            (sums[row].astype(F32) + grad[row * pad : row * pad + lon, cols].astype(F32)).astype(BF16) for row in range(rows)
        ]
        out[:, :, cols] = jnp.transpose(jnp.stack(done, axis=0), (1, 0, 2))

    order = (
        [("g", 0), ("a", 1), ("g", 1), ("g", 2), ("a", 2), ("g", 3), ("g", 4), ("f", 0), ("a", 3), ("f", 1)]
        + [("a", 4), ("f", 2), ("e", 0), ("f", 3), ("e", 1), ("f", 4), ("e", 2), ("e", 3), ("e", 4)]
    )
    if tiles != 5:
        order = [(what, k) for what in "gafe" for k in range(tiles) if (what, k) != ("a", 0)]
    def wait_sends():
        for k in range(tiles):
            for peer in peers:
                a_copy(peer, k, peer, me).wait_send()
                r_copy(peer, k, peer, me).wait_send()

            @pl.when(has_high)
            def _():
                up_copy(k).wait_send()

            @pl.when(has_low)
            def _():
                down_copy(k).wait_send()

    for what, k in order:
        if (what, k) == ("e", tiles - 1):
            wait_sends()
        {"g": make_gain, "a": analyze, "f": filter_tile, "e": finish}[what](k)


def on_device(parts, bands, conv_out, grad_out, w_in, b_in, w_out, basis_weight, filt, offsets):
    rows, lon, channels = conv_out.shape
    hidden = w_in.shape[1]
    assert parts == rows == REACH + 1 and LANES % parts == 0 and channels % LANES == 0
    modes2 = filt.shape[2]
    modes = modes2 // 2
    bases, width = filt.shape[0], rows + 2 * REACH
    assert filt.shape[1] <= 256 and modes2 % (16 * rows) == 0 and hidden % (2 * LANES) == 0
    analysis, synth = fourier_tables(parts * lon, modes)
    ana = np.ascontiguousarray(
        analysis.reshape(parts, lon, modes2).transpose(0, 2, 1)
    ).astype(ml_dtypes.bfloat16)
    tiles = channels // LANES
    pad = -(-lon // 16) * 16
    syn = np.zeros((parts, pad, modes2), ml_dtypes.bfloat16)
    syn[:, :lon] = synth.reshape(parts, lon, modes2)
    syn = syn.reshape(parts * pad, modes2)
    body = modes2 - modes2 // rows
    vmem = pl.BlockSpec(memory_space=pltpu.VMEM)
    hbm = pl.BlockSpec(memory_space=pl.ANY)
    dma = pltpu.SemaphoreType.DMA
    result = pl.pallas_call(
        functools.partial(kernel, parts, bands),
        out_shape=pltpu.VMEM((lon, rows, channels), BF16),
        in_specs=[hbm] * 10,
        out_specs=vmem,
        scratch_shapes=[
            pltpu.VMEM((lon, rows, channels), BF16),
            pltpu.VMEM((lon, rows, channels), BF16),
            pltpu.VMEM((rows * pad, channels), BF16),
            pltpu.VMEM((rows * pad, channels), BF16),
            pltpu.VMEM(w_in.shape, BF16),
            pltpu.VMEM(b_in.shape, F32),
            pltpu.VMEM(w_out.shape, BF16),
            pltpu.VMEM(basis_weight.shape, F32),
            pltpu.VMEM(filt.shape, BF16),
            pltpu.VMEM(offsets.shape, jnp.int32),
            pltpu.VMEM(ana.shape, BF16),
            pltpu.VMEM(syn.shape, BF16),
            pltpu.VMEM((rows * pad, hidden), F32),
            pltpu.VMEM((rows * pad, LANES), F32),
            pltpu.VMEM((rows * pad, hidden), BF16),
            pltpu.VMEM((parts, tiles, lon, LANES), BF16),
            pltpu.VMEM((tiles, parts, lon, LANES), BF16),
            pltpu.VMEM((tiles, modes2, LANES), BF16),
            pltpu.VMEM((2, tiles, body, LANES), BF16),
            pltpu.VMEM((tiles, body, LANES), BF16),
            pltpu.VMEM((tiles, body, LANES), BF16),
            pltpu.VMEM((modes2, LANES), BF16),
            pltpu.VMEM((modes2, LANES), BF16),
            pltpu.VMEM((tiles * SHIFTS, modes2, LANES), F32),
            pltpu.VMEM((modes2, 2 * bases * width), BF16),
            pltpu.VMEM((2 * bases * width, channels), F32),
            pltpu.VMEM((modes2, LANES), BF16),
            pltpu.VMEM((parts, tiles, lon, LANES), BF16),
            pltpu.VMEM((tiles, parts, lon, LANES), BF16),
            dma((parts, tiles)),
            dma((parts, tiles)),
            dma((2, tiles)),
            dma((2, tiles)),
            dma((parts, tiles)),
            dma((parts, tiles)),
            dma((11,)),
        ],
        compiler_params=pltpu.CompilerParams(
            collective_id=0, has_side_effects=True, vmem_limit_bytes=56 * 1024 * 1024
        ),
    )(jnp.transpose(conv_out, (1, 0, 2)), jnp.transpose(grad_out, (1, 0, 2)), w_in, b_in, w_out, basis_weight, filt, offsets,
      jnp.asarray(ana), jnp.asarray(syn))
    return jnp.transpose(result, (1, 0, 2))


def solution(mesh):
    grid = P(("member", "polar"), "azimuth", None)
    return jax.shard_map(
        functools.partial(on_device, mesh.shape["azimuth"], mesh.shape["polar"]),
        mesh=mesh,
        in_specs=(grid, grid, P(), P(), P(), P(), P(), P()),
        out_specs=grid,
        check_vma=False,
    )
```
